32 devices in a mesh: nodes: 16 (over z, y, x), rep: 2 (over core).
Axes of the slice: x: 2, y: 2, z: 4, core: 2. Of those that a mesh axis runs over, the one named last changes fastest.
Arguments:
- node_latent: bfloat16 [5120, 512], P(('nodes', 'rep')), may hold values from -6 to 6
- edge_saved: bfloat16 [40960, 512], P(('nodes', 'rep')), may hold values from -6 to 6
- node_cot: bfloat16 [5120, 512], P(('nodes', 'rep')), may hold values from -6 to 6
- edge_cot: bfloat16 [40960, 512], P(('nodes', 'rep')), may hold values from -6 to 6
- senders: int32 [40960], P(('nodes', 'rep')), may hold values from 0 to 447, as said below
- receivers: int32 [40960], P(('nodes', 'rep')), may hold values from 0 to 319
- ghost_rows: int32 [16, 16, 8], P('nodes'), may hold values from 0 to 319, as said below
- w_edge_in: bfloat16 [1536, 512], replicated, may hold values from -0.15625 to 0.15625
- w_edge_out: bfloat16 [512, 512], replicated, may hold values from -0.25 to 0.25
- edge_gain: float32 [512], replicated, may hold values from 0.5 to 2
- edge_offset: float32 [512], replicated, may hold values from -3 to 3
- w_node_in: bfloat16 [1024, 512], replicated, may hold values from -0.1875 to 0.1875
- w_node_out: bfloat16 [512, 512], replicated, may hold values from -0.25 to 0.25
- node_gain: float32 [512], replicated, may hold values from 0.5 to 2
Outputs:
- grad_nodes: bfloat16 [5120, 512], P(('nodes', 'rep'))
- grad_edges: bfloat16 [40960, 512], P(('nodes', 'rep'))
- grad_edge_in: bfloat16 [1536, 512], replicated
- grad_edge_out: bfloat16 [512, 512], replicated
- grad_node_in: bfloat16 [1024, 512], replicated
- grad_node_out: bfloat16 [512, 512], replicated
The draws below stay inside these ranges and needn't reach their ends.
Inputs may be any that keep to these rules, and one draw needn't show every extreme that they name: `senders`: A sender below 320 is a node of the edge's own partition; otherwise it is 320 + q * 8 + s, the ghost slot s of the list of a partition q other than the edge's own. Each list ghost_rows[q, p] holds 8 distinct rows.
All inputs are finite; a program needn't handle non-finite values.
Results may differ from the reference program's by a relative error of at most 0.008.
Values may be sent and summed in bfloat16 or wider, within the bound.
A program may use at most 128 MiB of HBM per device.

```python
import math
import jax
import jax.numpy as jnp
from jax import lax

D = 512
NODE_PART = 320
GP = 8
PARTITIONS = 16
NODES = 5120
EDGES = 40960
N_REP = 2


def draw_senders(key, part):
    key_list = jax.random.split(jax.random.fold_in(key, 11), 5)
    edge_index = jnp.arange(EDGES, dtype=jnp.int32)
    own_part = edge_index // (EDGES // PARTITIONS)
    live_count = jax.random.randint(key_list[0], (PARTITIONS, PARTITIONS), 1, GP + 1)
    live_count = live_count.at[0, 1].set(GP)
    offset = jax.random.randint(key_list[1], (EDGES,), 1, PARTITIONS)
    source = (own_part + offset) % PARTITIONS
    slot_index = jax.random.randint(key_list[2], (EDGES,), 0, 1 << 20) % live_count[source, own_part]
    local_row = jax.random.randint(key_list[3], (EDGES,), 0, NODE_PART)
    remote = jax.random.randint(key_list[4], (EDGES,), 0, 2)
    return jnp.where(remote == 1, NODE_PART + source * GP + slot_index, local_row).astype(jnp.int32)


def draw_ghost_rows(key, part):
    key_list = jax.random.split(jax.random.fold_in(key, 23), PARTITIONS * PARTITIONS)
    picked = jax.vmap(lambda one_key: jax.random.permutation(one_key, NODE_PART)[:GP])(key_list)
    return picked.reshape(PARTITIONS, PARTITIONS, GP).astype(jnp.int32)


def touch_ends(array, rng, least, high):
    longest = array.shape.index(max(array.shape))
    spots = []
    for shift in (0, 1):
        where = [jax.random.randint(jax.random.fold_in(rng, axis), (), 0, length) for axis, length in enumerate(array.shape)]
        where[longest] = (where[longest] + shift) % array.shape[longest]
        spots.append(tuple(where))
    return array.at[spots[0]].set(least).at[spots[1]].set(high)


def block_levels(rng, shape, pieces, least, high):
    factor_of, own = 1.0, jax.random.fold_in(rng, 6)
    for dim, blocks in pieces:
        steps = jnp.exp(jax.random.uniform(jax.random.fold_in(own, dim), (blocks,), jnp.float32, least / len(pieces), high / len(pieces)))
        factor_of = factor_of * jnp.repeat(steps, shape[dim] // blocks).reshape([-1 if axis == dim else 1 for axis in range(len(shape))])
    return factor_of


def noise(stream_key, dims, spread, bound, cuts=(), kind=jnp.bfloat16):
    factor_of = block_levels(stream_key, dims, cuts, -0.22, 0.18) if cuts else 1.0
    array = jax.random.normal(stream_key, dims, jnp.float32) * spread * factor_of
    return jnp.minimum(jnp.maximum(array, -bound), bound).astype(kind)


def setup_inputs(seed: int = 0) -> dict:
    key_of = jax.random.split(jax.random.key(seed), 15)
    return {
        "node_latent": noise(key_of[0], (NODES, D), 1.0, 6.0, ((0, 32),)),
        "edge_saved": noise(key_of[1], (EDGES, D), 1.0, 6.0, ((0, 32),)),
        "node_cot": noise(key_of[2], (NODES, D), 1.0, 6.0, ((0, 32),)),
        "edge_cot": noise(key_of[3], (EDGES, D), 1.0, 6.0, ((0, 32),)),
        "senders": draw_senders(jax.random.fold_in(key_of[14], 71), 0),
        "receivers": touch_ends(jax.random.randint(key_of[5], (EDGES,), 0, NODE_PART), jax.random.fold_in(key_of[5], 1), 0, NODE_PART - 1).astype(jnp.int32),
        "ghost_rows": draw_ghost_rows(jax.random.fold_in(key_of[14], 71), 0),
        "w_edge_in": noise(key_of[7], (3 * D, D), (3 * D) ** -0.5, 0.15625),
        "w_edge_out": noise(key_of[8], (D, D), D ** -0.5, 0.25),
        "edge_gain": jnp.clip(jnp.exp(jax.random.uniform(key_of[9], (D,), jnp.float32, math.log(0.5), math.log(2.0))), 0.5, 2.0),
        "edge_offset": noise(key_of[10], (D,), 0.5, 3.0, (), jnp.float32),
        "w_node_in": noise(key_of[11], (2 * D, D), (2 * D) ** -0.5, 0.1875),
        "w_node_out": noise(key_of[12], (D, D), D ** -0.5, 0.25),
        "node_gain": jnp.clip(jnp.exp(jax.random.uniform(key_of[13], (D,), jnp.float32, math.log(0.5), math.log(2.0))), 0.5, 2.0),
    }


EPS = 1e-05

def mat_mul(left, right):
    return jnp.dot(left, right, preferred_element_type=jnp.float32)

def mat_tn(left, right):
    return lax.dot_general(left, right, (((0,), (0,)), ((), ())), preferred_element_type=jnp.float32)

def mat_nt(left, right):
    return lax.dot_general(left, right, (((1,), (1,)), ((), ())), preferred_element_type=jnp.float32)

def silu_slope(value):
    sigmoid_v = jax.nn.sigmoid(value)
    return sigmoid_v * (1.0 + value * (1.0 - sigmoid_v))

def norm_forward(value):
    centred = value - lax.optimization_barrier(jnp.mean(value, axis=-1, keepdims=True))
    inverse = lax.rsqrt(lax.optimization_barrier(jnp.mean(centred * centred, axis=-1, keepdims=True)) + EPS)
    return (centred * inverse, inverse)

def norm_backward(grad_hat, normed, inverse):
    return inverse * (grad_hat - lax.optimization_barrier(jnp.mean(grad_hat, axis=-1, keepdims=True)) - normed * lax.optimization_barrier(jnp.mean(grad_hat * normed, axis=-1, keepdims=True)))

def edge_forward(edge_block, send_rows, recv_rows, w_edge_in, w_edge_out, edge_gain, edge_offset):
    latent_width = edge_block.shape[1]
    pre_act = mat_mul(edge_block, w_edge_in[:latent_width]) + mat_mul(send_rows, w_edge_in[latent_width:2 * latent_width]) + mat_mul(recv_rows, w_edge_in[2 * latent_width:])
    edge_hidden = jax.nn.silu(pre_act).astype(jnp.bfloat16)
    edge_normed, edge_inverse = norm_forward(mat_mul(edge_hidden, w_edge_out))
    message = edge_normed * edge_gain + edge_offset
    return (pre_act, edge_hidden, edge_normed, edge_inverse, message)

def edge_backward(edge_block, send_rows, recv_rows, edge_cot, message_grad, saved, w_edge_in, w_edge_out, edge_gain):
    pre_act, edge_hidden, edge_normed, edge_inverse = saved
    latent_width = edge_block.shape[1]
    grad_out = norm_backward(message_grad * edge_gain, edge_normed, edge_inverse).astype(jnp.bfloat16)
    grad_act = (mat_nt(grad_out, w_edge_out) * silu_slope(pre_act)).astype(jnp.bfloat16)
    in_grad = jnp.concatenate([mat_tn(edge_block, grad_act), mat_tn(send_rows, grad_act), mat_tn(recv_rows, grad_act)], 0)
    out_grad = mat_tn(edge_hidden, grad_out)
    edge_grad = (edge_cot.astype(jnp.float32) + mat_nt(grad_act, w_edge_in[:latent_width])).astype(jnp.bfloat16)
    send_grad = mat_nt(grad_act, w_edge_in[latent_width:2 * latent_width])
    recv_grad = mat_nt(grad_act, w_edge_in[2 * latent_width:])
    return (edge_grad, send_grad, recv_grad, in_grad, out_grad)

def node_pass(node_rows, totals_b, node_cot, w_node_in, w_node_out, node_gain):
    latent_width = node_rows.shape[1]
    node_pre = mat_mul(node_rows, w_node_in[:latent_width]) + mat_mul(totals_b, w_node_in[latent_width:])
    node_hidden = jax.nn.silu(node_pre).astype(jnp.bfloat16)
    node_normed, node_inverse = norm_forward(mat_mul(node_hidden, w_node_out))
    grad_out = norm_backward(node_cot.astype(jnp.float32) * node_gain, node_normed, node_inverse).astype(jnp.bfloat16)
    grad_act = (mat_nt(grad_out, w_node_out) * silu_slope(node_pre)).astype(jnp.bfloat16)
    in_grad = jnp.concatenate([mat_tn(node_rows, grad_act), mat_tn(totals_b, grad_act)], 0)
    direct_grad = mat_nt(grad_act, w_node_in[:latent_width])
    totals_grad = mat_nt(grad_act, w_node_in[latent_width:]).astype(jnp.bfloat16)
    return (direct_grad, totals_grad, in_grad, mat_tn(node_hidden, grad_out))

def reference(node_latent, edge_saved, node_cot, edge_cot, senders, receivers, ghost_rows, w_edge_in, w_edge_out, edge_gain, edge_offset, w_node_in, w_node_out, node_gain):
    latent_width = node_latent.shape[1]
    part_count = ghost_rows.shape[0]
    part_rows = node_latent.shape[0] // part_count
    part_edges = senders.shape[0] // part_count
    edge_latent = jnp.flip(edge_saved.reshape(part_count, N_REP, part_edges // N_REP, latent_width), axis=1).reshape(edge_saved.shape)
    global_ghost = (jnp.arange(part_count, dtype=jnp.int32)[:, None, None] * part_rows + ghost_rows).astype(jnp.int32)
    zero_sums = (jnp.zeros(w_edge_in.shape, jnp.float32), jnp.zeros(w_edge_out.shape, jnp.float32), jnp.zeros(w_node_in.shape, jnp.float32), jnp.zeros(w_node_out.shape, jnp.float32))

    def one_part(state_carry, part_index):
        grad_nodes, weight_sums = state_carry
        row_start = (part_index * part_rows).astype(jnp.int32)
        edge_start = (part_index * part_edges).astype(jnp.int32)
        part_latent = lax.dynamic_slice_in_dim(node_latent, row_start, part_rows, 0)
        ghost_index = lax.dynamic_index_in_dim(global_ghost, part_index, 1, keepdims=False).reshape(-1)
        node_table = jnp.concatenate([part_latent, node_latent[ghost_index]], 0)
        edge_block = lax.dynamic_slice_in_dim(edge_latent, edge_start, part_edges, 0)
        sender_block = lax.dynamic_slice_in_dim(senders, edge_start, part_edges, 0)
        receiver_block = lax.dynamic_slice_in_dim(receivers, edge_start, part_edges, 0)
        cot_block = lax.dynamic_slice_in_dim(edge_cot, edge_start, part_edges, 0)
        node_cot_block = lax.dynamic_slice_in_dim(node_cot, row_start, part_rows, 0)
        send_rows = node_table[sender_block]
        recv_rows = part_latent[receiver_block]
        pre_act, edge_hidden, edge_normed, edge_inverse, message = edge_forward(edge_block, send_rows, recv_rows, w_edge_in, w_edge_out, edge_gain, edge_offset)
        totals = jax.ops.segment_sum(message, receiver_block, num_segments=part_rows)
        direct_grad, totals_grad, node_in_grad, node_out_grad = node_pass(part_latent, totals.astype(jnp.bfloat16), node_cot_block, w_node_in, w_node_out, node_gain)
        message_grad = cot_block.astype(jnp.float32) + totals_grad[receiver_block].astype(jnp.float32)
        edge_grad, send_grad, recv_grad, edge_in_grad, edge_out_grad = edge_backward(edge_block, send_rows, recv_rows, cot_block, message_grad, (pre_act, edge_hidden, edge_normed, edge_inverse), w_edge_in, w_edge_out, edge_gain)
        table_grad = jax.ops.segment_sum(send_grad, sender_block, num_segments=part_rows + ghost_index.shape[0])
        row_grad = table_grad[:part_rows] + jax.ops.segment_sum(recv_grad, receiver_block, num_segments=part_rows) + direct_grad + node_cot_block.astype(jnp.float32)
        grad_nodes = grad_nodes.at[ghost_index].add(table_grad[part_rows:])
        grad_nodes = lax.dynamic_update_slice_in_dim(grad_nodes, lax.dynamic_slice_in_dim(grad_nodes, row_start, part_rows, 0) + row_grad, row_start, 0)
        weight_sums = (weight_sums[0] + edge_in_grad, weight_sums[1] + edge_out_grad, weight_sums[2] + node_in_grad, weight_sums[3] + node_out_grad)
        return ((grad_nodes, weight_sums), edge_grad)
    start_nodes = jnp.zeros(node_latent.shape, jnp.float32)
    (grad_nodes, weight_sums), edge_grads = lax.scan(one_part, (start_nodes, zero_sums), jnp.arange(part_count, dtype=jnp.int32))
    edge_scale = 1.0 / math.sqrt(EDGES)
    node_scale = 1.0 / math.sqrt(NODES)
    return (grad_nodes.astype(jnp.bfloat16), edge_grads.reshape(edge_saved.shape), (weight_sums[0] * edge_scale).astype(jnp.bfloat16), (weight_sums[1] * edge_scale).astype(jnp.bfloat16), (weight_sums[2] * node_scale).astype(jnp.bfloat16), (weight_sums[3] * node_scale).astype(jnp.bfloat16))
```

```python
import functools
import math

import jax
import jax.numpy as jnp
from jax import lax
from jax.experimental import pallas as pl
from jax.experimental.pallas import tpu as pltpu
from jax.sharding import PartitionSpec as P

EPS = 1e-05
F32 = jnp.float32
BF16 = jnp.bfloat16
MESH = pl.DeviceIdType.MESH
VMEM = pltpu.VMEM


def swapped(array):
    return lax.ppermute(array, "rep", [(0, 1), (1, 0)])


def mat_mul(left, right):
    return jnp.dot(left, right, preferred_element_type=F32)


def mat_tn(left, right):
    return lax.dot_general(left, right, (((0,), (0,)), ((), ())), preferred_element_type=F32)


def mat_nt(left, right):
    return lax.dot_general(left, right, (((1,), (1,)), ((), ())), preferred_element_type=F32)


def sigmoid(value):
    return 1.0 / (1.0 + jnp.exp(-value))


def norm_forward(value):
    centred = value - jnp.mean(value, axis=-1, keepdims=True)
    inverse = lax.rsqrt(jnp.mean(centred * centred, axis=-1, keepdims=True) + EPS)
    return (centred * inverse, inverse)


def norm_backward(grad_hat, normed, inverse):
    return inverse * (
        grad_hat
        - jnp.mean(grad_hat, axis=-1, keepdims=True)
        - normed * jnp.mean(grad_hat * normed, axis=-1, keepdims=True)
    )


def picks(index, shape, axis):
    return jnp.where(lax.broadcasted_iota(jnp.int32, shape, axis) == index, 1.0, 0.0).astype(BF16)


def forward_kernel(
    edge, s_col, r_col, r_row, table, w_in, w_out, gain, offset,
    pre_out, normed_out, inv_out, totals, proj,
):
    width = edge.shape[1]
    tile = edge.shape[0]
    table_rows = table.shape[0]
    part_rows = totals.shape[0]

    @pl.when(pl.program_id(0) == 0)
    def _():
        totals[...] = jnp.zeros_like(totals)
        proj[:table_rows] = mat_mul(table[...], w_in[width : 2 * width]).astype(BF16)
        proj[table_rows:] = mat_mul(table[:part_rows], w_in[2 * width :]).astype(BF16)

    pre = (
        mat_mul(edge[...], w_in[:width])
        + mat_mul(picks(s_col[...], (tile, table_rows), 1), proj[:table_rows])
        + mat_mul(picks(r_col[...], (tile, part_rows), 1), proj[table_rows:])
    )
    pre_out[...] = pre
    hidden = (pre * sigmoid(pre)).astype(BF16)
    normed, inverse = norm_forward(mat_mul(hidden, w_out[...]))
    normed_out[...] = normed.astype(BF16)
    inv_out[...] = inverse
    message = (normed * gain[...] + offset[...]).astype(BF16)
    totals[...] += mat_mul(picks(r_row[...], (part_rows, tile), 0), message)


def node_kernel(
    scale, own, other, latent, cot, w_in, w_out, gain, totals_grad, base, w_grads
):
    width = latent.shape[1]
    half = latent.shape[0] // 2
    totals_b = (
        own[...] + jnp.concatenate([other[half:], other[:half]], 0)
    ).astype(BF16)
    rows = latent[...]
    pre = mat_mul(rows, w_in[:width]) + mat_mul(totals_b, w_in[width:])
    sig = sigmoid(pre)
    hidden = (pre * sig).astype(BF16)
    normed, inverse = norm_forward(mat_mul(hidden, w_out[...]))
    cots = cot[...].astype(F32)
    grad_out = norm_backward(cots * gain[...], normed, inverse).astype(BF16)
    grad_act = (mat_nt(grad_out, w_out[...]) * (sig * (1.0 + pre * (1.0 - sig)))).astype(BF16)
    totals_grad[...] = mat_nt(grad_act, w_in[width:]).astype(BF16)
    base[...] = mat_nt(grad_act[:half], w_in[:width]) + cots[:half]
    w_grads[:width] = (mat_tn(rows[:half], grad_act[:half]) * scale).astype(BF16)
    w_grads[width : 2 * width] = (mat_tn(totals_b[:half], grad_act[:half]) * scale).astype(BF16)
    w_grads[2 * width :] = (mat_tn(hidden[:half], grad_out[:half]) * scale).astype(BF16)


def backward_kernel(
    scale, edge, cot, pre_in, normed_in, inv_in, s_row, r_row, r_col,
    table, t_grad, w_in, w_out, gain, node_w,
    edge_grad, w_grads, row_grad, ghost_grad,
    acc_edge, acc_out, acc_send, acc_recv,
):
    width = edge.shape[1]
    tile = edge.shape[0]
    table_rows = table.shape[0]
    part_rows = t_grad.shape[0]

    @pl.when(pl.program_id(0) == 0)
    def _():
        acc_edge[...] = jnp.zeros_like(acc_edge)
        acc_out[...] = jnp.zeros_like(acc_out)
        acc_send[...] = jnp.zeros_like(acc_send)
        acc_recv[...] = jnp.zeros_like(acc_recv)

    cots = cot[...].astype(F32)
    message_grad = cots + mat_mul(picks(r_col[...], (tile, part_rows), 1), t_grad[...])
    grad_out = norm_backward(
        message_grad * gain[...], normed_in[...].astype(F32), inv_in[...]
    ).astype(BF16)
    pre = pre_in[...]
    sig = sigmoid(pre)
    hidden = (pre * sig).astype(BF16)
    grad_act = (mat_nt(grad_out, w_out[...]) * (sig * (1.0 + pre * (1.0 - sig)))).astype(BF16)
    edge_grad[...] = (cots + mat_nt(grad_act, w_in[:width])).astype(BF16)
    acc_edge[...] += mat_tn(edge[...], grad_act)
    acc_out[...] += mat_tn(hidden, grad_out)
    acc_send[...] += mat_mul(picks(s_row[...], (table_rows, tile), 0), grad_act)
    acc_recv[...] += mat_mul(picks(r_row[...], (part_rows, tile), 0), grad_act)

    @pl.when(pl.program_id(0) == pl.num_programs(0) - 1)
    def _():
        send = acc_send[...].astype(BF16)
        recv = acc_recv[...].astype(BF16)
        table_grad = mat_nt(send, w_in[width : 2 * width])
        row_grad[...] = table_grad[:part_rows] + mat_nt(recv, w_in[2 * width :])
        ghost_grad[...] = table_grad[part_rows:].astype(BF16)
        w_grads[:width] = (acc_edge[...] * scale).astype(BF16)
        w_grads[width : 2 * width] = (mat_tn(table[...], send) * scale).astype(BF16)
        w_grads[2 * width : 3 * width] = (mat_tn(table[:part_rows], recv) * scale).astype(BF16)
        w_grads[3 * width : 4 * width] = (acc_out[...] * scale).astype(BF16)
        w_grads[4 * width :] = node_w[...]


def orders(bits):
    return (
        tuple(range(bits)),
        tuple(b ^ 1 if (b ^ 1) < bits else b for b in range(bits)),
    )


def reduce_kernel(
    nodes, cuts, x, out, pair, acc, stage, landed,
    pair_sem, rs_sem, ag_sem, fw_sem,
):
    bits = nodes.bit_length() - 1
    me = lax.axis_index("nodes")
    rep = lax.axis_index("rep")
    other_rep = 1 - rep
    mine = [(me // (1 << b)) % 2 for b in range(bits)]
    flip = [(1 << b) * (1 - 2 * mine[b]) for b in range(bits)]
    streams = orders(bits)
    cols = [slice(*cut) for cut in cuts]

    def place(s, v):
        spot = me
        for k, b in enumerate(streams[s]):
            spot = spot + flip[b] * ((v // (1 << (bits - 1 - k))) % 2)
        return spot

    def partner(b):
        return {"nodes": me + flip[b]}

    barrier = pltpu.get_barrier_semaphore()
    for b in range(bits):
        pl.semaphore_signal(barrier, inc=1, device_id=partner(b), device_id_type=MESH)
    pl.semaphore_signal(barrier, inc=1, device_id={"rep": other_rep}, device_id_type=MESH)
    pl.semaphore_wait(barrier, bits + 1)

    first = []
    for s in range(2):
        copy = pltpu.make_async_remote_copy(
            src_ref=x.at[pl.ds(other_rep * nodes, nodes), :, cols[s]],
            dst_ref=pair.at[:, :, cols[s]],
            send_sem=pair_sem.at[0, s],
            recv_sem=pair_sem.at[1, s],
            device_id={"rep": other_rep},
            device_id_type=MESH,
        )
        copy.start()
        first.append(copy)

    def halve(s, k):
        half = nodes >> (k + 1)
        copy = pltpu.make_async_remote_copy(
            src_ref=stage.at[pl.ds(half, half), :, cols[s]],
            dst_ref=landed.at[pl.ds(half, half), :, cols[s]],
            send_sem=rs_sem.at[0, s, k],
            recv_sem=rs_sem.at[1, s, k],
            device_id=partner(streams[s][k]),
            device_id_type=MESH,
        )
        copy.start()
        return copy

    half = nodes // 2
    copies = {}
    for s in range(2):
        first[s].wait_recv()

        def load(v):
            spot = place(s, v)
            return x[rep * nodes + spot, :, cols[s]].astype(F32) + pair[spot, :, cols[s]].astype(F32)

        @pl.loop(half, nodes)
        def _(v):
            stage[v, :, cols[s]] = load(v).astype(BF16)

        copies[s, 0] = halve(s, 0)

    for s in range(2):

        def load(v):
            spot = place(s, v)
            return x[rep * nodes + spot, :, cols[s]].astype(F32) + pair[spot, :, cols[s]].astype(F32)

        @pl.loop(0, half)
        def _(v):
            acc[v, :, cols[s]] = load(v)

    for k in range(bits):
        half = nodes >> (k + 1)
        for s in range(2):
            copies[s, k].wait_recv()
            if k + 1 < bits:
                quarter = half // 2

                @pl.loop(quarter, half)
                def _(v):
                    stage[v, :, cols[s]] = (
                        acc[v, :, cols[s]] + landed[half + v, :, cols[s]].astype(F32)
                    ).astype(BF16)

                copies[s, k + 1] = halve(s, k + 1)

                @pl.loop(0, quarter)
                def _(v):
                    acc[v, :, cols[s]] = acc[v, :, cols[s]] + landed[half + v, :, cols[s]].astype(F32)
            else:
                out[rep * nodes + me, :, cols[s]] = (
                    acc[0, :, cols[s]] + landed[1, :, cols[s]].astype(F32)
                ).astype(BF16)

    def hand_on(s, v, sems, slot, device):
        spot = rep * nodes + place(s, v)
        copy = pltpu.make_async_remote_copy(
            src_ref=out.at[spot, :, cols[s]],
            dst_ref=out.at[spot, :, cols[s]],
            send_sem=sems.at[0, s, slot],
            recv_sem=sems.at[1, s, slot],
            device_id=device,
            device_id_type=MESH,
        )
        copy.start()
        return copy

    spread, forward = {}, {}
    for s in range(2):
        b = streams[s][bits - 1]
        spread[s, 1] = hand_on(s, 0, ag_sem, 1, partner(b))
        forward[s, 0] = hand_on(s, 0, fw_sem, 0, {"rep": other_rep})
    for k in range(bits - 1, -1, -1):
        half = nodes >> (k + 1)
        for s in range(2):
            for v in range(half, 2 * half):
                spot = rep * nodes + place(s, v)
                pltpu.make_async_remote_copy(
                    src_ref=out.at[spot, :, cols[s]],
                    dst_ref=out.at[spot, :, cols[s]],
                    send_sem=ag_sem.at[0, s, v],
                    recv_sem=ag_sem.at[1, s, v],
                    device_id=partner(streams[s][k]),
                    device_id_type=MESH,
                ).wait_recv()
            if k > 0:
                for v in range(2 * half):
                    slot = 2 * half + v
                    spread[s, slot] = hand_on(s, v, ag_sem, slot, partner(streams[s][k - 1]))
            for v in range(half, 2 * half):
                forward[s, v] = hand_on(s, v, fw_sem, v, {"rep": other_rep})
    for copy in forward.values():
        copy.wait_recv()
    for copy in [*first, *copies.values(), *spread.values(), *forward.values()]:
        copy.wait_send()


def reduced(x, nodes):
    count, rows, width = x.shape
    cuts = ((0, width // 2), (width // 2, width))
    bits = nodes.bit_length() - 1
    return pl.pallas_call(
        functools.partial(reduce_kernel, nodes, cuts),
        out_shape=jax.ShapeDtypeStruct(x.shape, BF16),
        in_specs=[pl.BlockSpec(memory_space=VMEM)],
        out_specs=pl.BlockSpec(memory_space=VMEM),
        scratch_shapes=[
            VMEM((nodes, rows, width), BF16),
            VMEM((nodes // 2, rows, width), F32),
            VMEM((nodes, rows, width), BF16),
            VMEM((nodes, rows, width), BF16),
            pltpu.SemaphoreType.DMA((2, 2)),
            pltpu.SemaphoreType.DMA((2, 2, bits)),
            pltpu.SemaphoreType.DMA((2, 2, nodes)),
            pltpu.SemaphoreType.DMA((2, 2, nodes)),
        ],
        compiler_params=pltpu.CompilerParams(collective_id=0, has_side_effects=True),
        name="weight_sum",
    )(x)


def whole():
    return pl.BlockSpec(memory_space=VMEM)


def shards(
    node_latent, edge_saved, node_cot, edge_cot, senders, receivers, ghost_rows,
    w_edge_in, w_edge_out, edge_gain, edge_offset, w_node_in, w_node_out, node_gain,
):
    width = node_latent.shape[1]
    own_rows = node_latent.shape[0]
    part_rows = 2 * own_rows
    edges = senders.shape[0]
    node_count = lax.axis_size("nodes")
    rep = lax.axis_index("rep")
    tile = 256
    tiles = edges // tile
    edge_scale = 1.0 / math.sqrt(edges * node_count * 2)
    node_scale = 1.0 / math.sqrt(own_rows * node_count * 2)

    def local(index):
        turned = (index + own_rows * rep) % part_rows
        return jnp.where(index < part_rows, turned, index)

    both = swapped(jnp.concatenate([node_latent, node_cot], 0))
    latent = jnp.concatenate([node_latent, both[:own_rows]], 0)
    cots = jnp.concatenate([node_cot, both[own_rows:]], 0)
    edge_latent = swapped(edge_saved)
    lists = local(ghost_rows[0])
    part_count, slots = lists.shape
    ghost_count = part_count * slots
    flat = lists.reshape(-1)
    outgoing = latent[flat].reshape(part_count, slots, width)
    ghosts = lax.all_to_all(outgoing, "nodes", split_axis=0, concat_axis=0, tiled=True)
    table = jnp.concatenate([latent, ghosts.reshape(ghost_count, width)], 0)
    table_rows = part_rows + ghost_count
    send = local(senders)
    recv = local(receivers)
    s_col, r_col = send[:, None], recv[:, None]
    s_row, r_row = send[None, :], recv[None, :]
    gain = edge_gain[None, :]

    edge_spec = pl.BlockSpec((tile, width), lambda i: (i, 0))
    col_spec = pl.BlockSpec((tile, 1), lambda i: (i, 0))
    row_spec = pl.BlockSpec((1, tile), lambda i: (0, i))
    params = pltpu.CompilerParams(dimension_semantics=("arbitrary",))

    pre, normed, inverse, partial_totals = pl.pallas_call(
        forward_kernel,
        grid=(tiles,),
        out_shape=(
            jax.ShapeDtypeStruct((edges, width), F32),
            jax.ShapeDtypeStruct((edges, width), BF16),
            jax.ShapeDtypeStruct((edges, 1), F32),
            jax.ShapeDtypeStruct((part_rows, width), F32),
        ),
        in_specs=[edge_spec, col_spec, col_spec, row_spec] + [whole()] * 5,
        out_specs=(edge_spec, edge_spec, col_spec, whole()),
        scratch_shapes=[VMEM((table_rows + part_rows, width), BF16)],
        compiler_params=params,
        name="edge_forward",
    )(edge_latent, s_col, r_col, r_row, table, w_edge_in, w_edge_out, gain, edge_offset[None, :])

    totals_grad, base, node_w = pl.pallas_call(
        functools.partial(node_kernel, node_scale),
        out_shape=(
            jax.ShapeDtypeStruct((part_rows, width), BF16),
            jax.ShapeDtypeStruct((own_rows, width), F32),
            jax.ShapeDtypeStruct((3 * width, width), BF16),
        ),
        in_specs=[whole()] * 7,
        out_specs=(whole(),) * 3,
        name="node_pass",
    )(
        partial_totals, swapped(partial_totals), latent, cots,
        w_node_in, w_node_out, node_gain[None, :],
    )

    edge_grad, w_grads, row_grad, ghost_grad = pl.pallas_call(
        functools.partial(backward_kernel, edge_scale),
        grid=(tiles,),
        out_shape=(
            jax.ShapeDtypeStruct((edges, width), BF16),
            jax.ShapeDtypeStruct((7 * width, width), BF16),
            jax.ShapeDtypeStruct((part_rows, width), F32),
            jax.ShapeDtypeStruct((ghost_count, width), BF16),
        ),
        in_specs=[edge_spec, edge_spec, edge_spec, edge_spec, col_spec, row_spec, row_spec, col_spec]
        + [whole()] * 6,
        out_specs=(edge_spec, whole(), whole(), whole()),
        scratch_shapes=[
            VMEM((width, width), F32),
            VMEM((width, width), F32),
            VMEM((table_rows, width), F32),
            VMEM((part_rows, width), F32),
        ],
        compiler_params=params,
        name="edge_backward",
    )(
        edge_latent, edge_cot, pre, normed, inverse, s_row, r_row, r_col,
        table, totals_grad, w_edge_in, w_edge_out, gain, node_w,
    )

    returned = lax.all_to_all(
        ghost_grad.reshape(part_count, slots, width), "nodes", split_axis=0, concat_axis=0, tiled=True
    ).reshape(ghost_count, width)
    taken = (lax.broadcasted_iota(jnp.int32, (part_rows, ghost_count), 0) == flat[None, :]).astype(BF16)
    row_grad = row_grad + mat_mul(taken, returned)
    grad_nodes = (row_grad[:own_rows] + swapped(row_grad[own_rows:]) + base).astype(BF16)

    devices = 2 * node_count
    total = reduced(w_grads.reshape(devices, 7 * width // devices, width), node_count)
    total = total.reshape(7 * width, width)
    return (
        grad_nodes,
        edge_grad,
        total[: 3 * width],
        total[3 * width : 4 * width],
        total[4 * width : 6 * width],
        total[6 * width :],
    )


def solution(mesh):
    return jax.shard_map(
        shards,
        mesh=mesh,
        in_specs=(
            P(("nodes", "rep"), None),
            P(("nodes", "rep"), None),
            P(("nodes", "rep"), None),
            P(("nodes", "rep"), None),
            P(("nodes", "rep")),
            P(("nodes", "rep")),
            P("nodes", None, None),
            P(),
            P(),
            P(),
            P(),
            P(),
            P(),
            P(),
        ),
        out_specs=(P(("nodes", "rep"), None), P(("nodes", "rep"), None), P(), P(), P(), P()),
        check_vma=False,
    )
```
